512 devices in a mesh: row: 32 (over z, y_lo), col: 16 (over x, y_hi, core).
Axes of the slice: x: 4, y: 4 (y_hi: 2, y_lo: 2; y = y_hi * 2 + y_lo), z: 16, core: 2. Of those that a mesh axis runs over, the one named last changes fastest.
Arguments:
- covariance: float32 [12288, 12288], P('col', 'row'), as said below
- courant_x: float32 [8, 96, 128], replicated, may hold values from -0.4 to 0.4
- courant_y: float32 [8, 96, 128], replicated, may hold values from -0.4 to 0.4
- wind_index: int32 [4], replicated, may hold values from 0 to 7
Outputs:
- forecast: float32 [12288, 12288], P(('row', 'col'))
The draws below stay inside these ranges and needn't reach their ends.
Inputs may be any that keep to these rules, and one draw needn't show every extreme that they name: covariance is exactly symmetric.
All inputs are finite; a program needn't handle non-finite values.
Results may differ from the reference program's by a relative error of at most 0.00002.
Values sent between devices are 32-bit elements; how exact they have to be, the bound alone decides.
No kernel may reach another device: no remote copies, remote signals or barrier semaphores. Data moves between devices by JAX's collectives and lax.ppermute only.
A program may use at most 64 MiB of HBM per device.

```python
import jax
import jax.numpy as jnp
from jax import lax

NLAT = 96
NLON = 128
STEPS = 4
WINDS = 8


def draw_covariance(key, part):
    states_count = NLAT * NLON
    randoms = jax.random.normal(key, (states_count, states_count), jnp.float32)
    symmetric = 0.5 * (randoms + randoms.T)
    return symmetric + 2.0 * jnp.eye(states_count, dtype=jnp.float32)


def place_ends(values, stream_key, smallest, largest):
    place = [jax.random.randint(jax.random.fold_in(stream_key, axis), (), 0, length) for axis, length in enumerate(values.shape)]
    widest = values.shape.index(max(values.shape))
    neighbour = place[:widest] + [(place[widest] + 1) % values.shape[widest]] + place[widest + 1:]
    return values.at[tuple(place)].set(smallest).at[tuple(neighbour)].set(largest)


def setup_inputs(seed: int = 0) -> dict:
    arg_keys = jax.random.split(jax.random.key(seed), 5)
    return {
        "covariance": draw_covariance(jax.random.fold_in(arg_keys[4], 71), 0),
        "courant_x": jnp.clip(jax.random.uniform(arg_keys[1], (WINDS, NLAT, NLON), jnp.float32, -0.4, 0.4), -0.4, 0.4),
        "courant_y": jnp.clip(jax.random.uniform(arg_keys[2], (WINDS, NLAT, NLON), jnp.float32, -0.4, 0.4), -0.4, 0.4),
        "wind_index": place_ends(jax.random.randint(arg_keys[3], (STEPS,), 0, WINDS), jax.random.fold_in(arg_keys[3], 1), 0, WINDS - 1).astype(jnp.int32),
    }


diffusivity = 0.05
block_count = 16


def advance(states, flow_east, flow_north):
    eastern = jnp.roll(states, -1, axis=2)
    western = jnp.roll(states, 1, axis=2)
    zeros_row = jnp.zeros_like(states[:, :1, :])
    northern = jnp.concatenate([states[:, 1:, :], zeros_row], axis=1)
    southern = jnp.concatenate([zeros_row, states[:, :-1, :]], axis=1)
    upwind = jnp.maximum(flow_east, 0.0) * (states - western) + jnp.minimum(flow_east, 0.0) * (eastern - states)
    upwind = upwind + jnp.maximum(flow_north, 0.0) * (states - southern) + jnp.minimum(flow_north, 0.0) * (northern - states)
    return states - upwind + diffusivity * (eastern + western + northern + southern - 4.0 * states)


def propagate(states, courant_x, courant_y, wind_index):
    def advance_once(counter, current):
        chosen = wind_index[counter]
        flow_east = lax.dynamic_index_in_dim(courant_x, chosen, 0, keepdims=False)
        flow_north = lax.dynamic_index_in_dim(courant_y, chosen, 0, keepdims=False)
        return advance(current, flow_east, flow_north)

    return lax.fori_loop(0, wind_index.shape[0], advance_once, states)


def propagate_rows(matrix, courant_x, courant_y, wind_index):
    cells_all = NLAT * NLON
    blocks = matrix.reshape(block_count, cells_all // block_count, NLAT, NLON)
    result = lax.map(lambda block_rows: propagate(block_rows, courant_x, courant_y, wind_index), blocks)
    return result.reshape(cells_all, cells_all)


def reference(covariance, courant_x, courant_y, wind_index):
    propagated_t = propagate_rows(covariance.T, courant_x, courant_y, wind_index)
    return propagate_rows(propagated_t.T, courant_x, courant_y, wind_index)
```

```python
import functools

import jax
import jax.numpy as jnp
from jax import lax
from jax.experimental import pallas as pl
from jax.experimental.pallas import tpu as pltpu
from jax.sharding import Mesh, PartitionSpec as P

NLAT = 96
NLON = 128
STEPS = 4
HALO = STEPS
DIFFUSIVITY = 0.05
LATS_DEV = 3
LATS_PLANE = 2 * LATS_DEV
WINDOW = LATS_PLANE + 2 * HALO


def coef_kernel(wind_ref, cx_ref, cy_ref, out_ref):
    flow_east = cx_ref[0]
    flow_north = cy_ref[0]
    east_pos = jnp.maximum(flow_east, 0.0)
    east_neg = jnp.minimum(flow_east, 0.0)
    north_pos = jnp.maximum(flow_north, 0.0)
    north_neg = jnp.minimum(flow_north, 0.0)
    centre = 1.0 - 4.0 * DIFFUSIVITY - (east_pos - east_neg) - (north_pos - north_neg)
    parts = (
        centre,
        east_pos + DIFFUSIVITY,
        DIFFUSIVITY - east_neg,
        north_pos + DIFFUSIVITY,
        DIFFUSIVITY - north_neg,
    )
    out_ref[...] = jnp.zeros_like(out_ref)
    for k, part in enumerate(parts):
        out_ref[0, pl.ds(8 * HALO + k, NLAT, stride=8), :] = part


def coefficients(courant_x, courant_y, wind_index):
    rows = 8 * (NLAT + 2 * HALO)
    out = pl.pallas_call(
        coef_kernel,
        grid_spec=pltpu.PrefetchScalarGridSpec(
            num_scalar_prefetch=1,
            grid=(STEPS,),
            in_specs=[
                pl.BlockSpec((1, NLAT, NLON), lambda s, wind: (wind[s], 0, 0)),
                pl.BlockSpec((1, NLAT, NLON), lambda s, wind: (wind[s], 0, 0)),
            ],
            out_specs=pl.BlockSpec((1, rows, NLON), lambda s, wind: (s, 0, 0)),
        ),
        out_shape=jax.ShapeDtypeStruct((STEPS, rows, NLON), jnp.float32),
        compiler_params=pltpu.CompilerParams(vmem_limit_bytes=24 << 20),
        name="coefs",
    )(wind_index, courant_x, courant_y)
    return out.reshape(STEPS, NLAT + 2 * HALO, 8, NLON)


def stencil(coef, x, south, north):
    west = pltpu.roll(x, 1, 1)
    east = pltpu.roll(x, NLON - 1, 1)
    return (
        x * coef[0:1]
        + west * coef[1:2]
        + east * coef[2:3]
        + (south * coef[3:4] + north * coef[4:5])
    )


def left_kernel(place_ref, coef_ref, own, pair, big1, small1, big2, small2, out_ref, w0, w1):
    z = place_ref[0]
    yl = place_ref[1]
    for i in range(LATS_DEV):
        lanes = slice(i * NLON, (i + 1) * NLON)
        w0[HALO + LATS_DEV * yl + i] = own[:, lanes]
        w0[HALO + LATS_DEV - LATS_DEV * yl + i] = pair[:, lanes]
        w0[10 - 9 * yl + i] = big1[:, lanes]
        w0[1 + 9 * yl + i] = big2[:, lanes]
    w0[13 * yl] = small1[...]
    w0[13 - 13 * yl] = small2[...]
    bufs = (w0, w1)
    for s in range(STEPS):
        src, dst = bufs[s % 2], bufs[(s + 1) % 2]

        def body(p, carry, s=s, src=src, dst=dst):
            coef = coef_ref[s, LATS_PLANE * z + p]
            new = stencil(coef, src[p], src[p - 1], src[p + 1])
            if s == STEPS - 1:
                out_ref[pl.ds(pl.multiple_of((p - HALO) * NLON, NLON), NLON), :] = new.T
            else:
                dst[p] = new
            return carry

        lax.fori_loop(s + 1, WINDOW - 1 - s, body, 0)


def right_kernel(coef_ref, got_ref, out_ref, b0, b1):
    rows = out_ref.shape[0]
    half = got_ref.shape[0] // 2
    zero = jnp.zeros((rows, NLON), jnp.float32)
    for buf in (b0, b1):
        buf[0] = zero
        buf[NLAT + 1] = zero

    def gather(c, carry):
        for yl in range(2):
            for i in range(LATS_DEV):
                b0[1 + c * LATS_PLANE + yl * LATS_DEV + i] = got_ref[
                    yl * half + c, :, i * NLON : (i + 1) * NLON
                ]
        return carry

    lax.fori_loop(0, half, gather, 0)
    bufs = (b0, b1)
    unroll = 8
    for s in range(STEPS):
        src, dst = bufs[s % 2], bufs[(s + 1) % 2]

        def body(j, carry, s=s, src=src, dst=dst):
            for i in range(unroll):
                lat = j * unroll + i
                new = stencil(coef_ref[s, lat + HALO], src[lat + 1], src[lat], src[lat + 2])
                if s == STEPS - 1:
                    out_ref[:, pl.ds(pl.multiple_of(lat * NLON, NLON), NLON)] = new
                else:
                    dst[lat + 1] = new
            return carry

        lax.fori_loop(0, NLAT // unroll, body, 0)


def shards(covariance, courant_x, courant_y, wind_index):
    planes = lax.axis_size("z")
    yl = lax.axis_index("yl")
    z = lax.axis_index("z")
    place = jnp.stack([z, yl]).astype(jnp.int32)
    cols = covariance.shape[0] // 2
    row = ("z", "yl")
    swap = [(r, r ^ 1) for r in range(2 * planes)]
    outward = [(r, r + (2 if r % 2 else -2)) for r in range(2 * planes)]
    outward = [(a, b) for a, b in outward if 0 <= b < 2 * planes]
    inward = [(b, a) for a, b in outward]

    other = lax.dynamic_slice_in_dim(covariance, (1 - yl) * cols, cols, 0)
    own = lax.dynamic_slice_in_dim(covariance, yl * cols, cols, 0)
    pair = lax.ppermute(other, row, swap)
    big1 = lax.ppermute(own, row, outward)
    small1 = lax.ppermute(
        lax.dynamic_slice_in_dim(own, (1 - yl) * 2 * NLON, NLON, 1), row, inward
    )
    big2 = lax.ppermute(pair, row, inward)
    small2 = lax.ppermute(lax.dynamic_slice_in_dim(pair, yl * 2 * NLON, NLON, 1), row, outward)

    coefs = coefficients(courant_x, courant_y, wind_index)

    window = pltpu.VMEM((WINDOW, cols, NLON), jnp.float32)
    vmem = pl.BlockSpec(memory_space=pltpu.VMEM)
    propagated = pl.pallas_call(
        left_kernel,
        in_specs=[pl.BlockSpec(memory_space=pltpu.SMEM)] + [vmem] * 7,
        out_specs=vmem,
        out_shape=jax.ShapeDtypeStruct((LATS_PLANE * NLON, cols), jnp.float32),
        scratch_shapes=[window, window],
        compiler_params=pltpu.CompilerParams(vmem_limit_bytes=24 << 20),
        name="left",
    )(place, coefs, own, pair, big1, small1, big2, small2)

    group = ("yl", "x", "yh", "core")
    members = 2 * lax.axis_size("x") * lax.axis_size("yh") * lax.axis_size("core")
    rows_dev = propagated.shape[0] // members
    sent = propagated.reshape(members, rows_dev, cols)
    got = lax.all_to_all(sent, group, split_axis=0, concat_axis=0, tiled=True)

    state = pltpu.VMEM((NLAT + 2, rows_dev, NLON), jnp.float32)
    return pl.pallas_call(
        right_kernel,
        in_specs=[vmem, vmem],
        out_specs=vmem,
        out_shape=jax.ShapeDtypeStruct((rows_dev, NLAT * NLON), jnp.float32),
        scratch_shapes=[state, state],
        compiler_params=pltpu.CompilerParams(vmem_limit_bytes=24 << 20),
        name="right",
    )(coefs, got)


def solution(mesh):
    inner = Mesh(mesh.devices.reshape(16, 2, 4, 2, 2), ("z", "yl", "x", "yh", "core"))
    row, col = ("z", "yl"), ("x", "yh", "core")
    placed = (P(col, row), P(), P(), P())
    return jax.shard_map(
        shards, mesh=inner, in_specs=placed, out_specs=P(row + col, None), check_vma=False
    )
```

```python
import jax
import jax.numpy as jnp
from jax import lax
from jax.experimental import pallas as pl
from jax.experimental.pallas import tpu as pltpu
from jax.sharding import Mesh, PartitionSpec as P


NLAT = 96
NLON = 128
STEPS = 4
HALO = STEPS
DIFFUSIVITY = 0.05
LATS_DEV = 3
LATS_PLANE = 2 * LATS_DEV
WINDOW = LATS_PLANE + 2 * HALO
PARTS = (192, 192)
VMEM_LIMIT = 24 << 20


def coef_kernel(wind_ref, cx_ref, cy_ref, out_ref):
    flow_east = cx_ref[0]
    flow_north = cy_ref[0]
    east_pos = jnp.maximum(flow_east, 0.0)
    east_neg = jnp.minimum(flow_east, 0.0)
    north_pos = jnp.maximum(flow_north, 0.0)
    north_neg = jnp.minimum(flow_north, 0.0)
    centre = 1.0 - 4.0 * DIFFUSIVITY - (east_pos - east_neg) - (north_pos - north_neg)
    parts = (
        centre,
        east_pos + DIFFUSIVITY,
        DIFFUSIVITY - east_neg,
        north_pos + DIFFUSIVITY,
        DIFFUSIVITY - north_neg,
    )
    out_ref[...] = jnp.zeros_like(out_ref)
    for k, part in enumerate(parts):
        out_ref[0, pl.ds(8 * HALO + k, NLAT, stride=8), :] = part


def coefficients(courant_x, courant_y, wind_index):
    rows = 8 * (NLAT + 2 * HALO)
    out = pl.pallas_call(
        coef_kernel,
        grid_spec=pltpu.PrefetchScalarGridSpec(
            num_scalar_prefetch=1,
            grid=(STEPS,),
            in_specs=[
                pl.BlockSpec((1, NLAT, NLON), lambda s, wind: (wind[s], 0, 0)),
                pl.BlockSpec((1, NLAT, NLON), lambda s, wind: (wind[s], 0, 0)),
            ],
            out_specs=pl.BlockSpec((1, rows, NLON), lambda s, wind: (s, 0, 0)),
        ),
        out_shape=jax.ShapeDtypeStruct((STEPS, rows, NLON), jnp.float32),
        compiler_params=pltpu.CompilerParams(vmem_limit_bytes=VMEM_LIMIT),
        name="coefs",
    )(wind_index, courant_x, courant_y)
    return out.reshape(STEPS, NLAT + 2 * HALO, 8, NLON)


def stencil(coef, x, south, north):
    west = pltpu.roll(x, 1, 1)
    east = pltpu.roll(x, NLON - 1, 1)
    return (
        x * coef[0:1]
        + west * coef[1:2]
        + east * coef[2:3]
        + (south * coef[3:4] + north * coef[4:5])
    )


def lanes_of(yl, j):
    i = LATS_DEV - 1 - j + yl * (2 * j - LATS_DEV + 1)
    return pl.ds(pl.multiple_of(i * NLON, NLON), NLON)


def place_of(yl, q):
    return WINDOW - 1 - q + yl * (2 * q - WINDOW + 1)


def mirrored(coef_ref, place_ref, s, q, x, before, after):
    z = place_ref[0]
    yl = place_ref[1]
    lat = LATS_PLANE * z + place_of(yl, q)
    west = pltpu.roll(x, 1, 1)
    east = pltpu.roll(x, NLON - 1, 1)
    return (
        x * coef_ref[s, lat, 0:1, :]
        + west * coef_ref[s, lat, 1:2, :]
        + east * coef_ref[s, lat, 2:3, :]
        + (
            before * coef_ref[s, lat, pl.ds(4 - yl, 1), :]
            + after * coef_ref[s, lat, pl.ds(3 + yl, 1), :]
        )
    )


EARLY = [(s, q) for s in range(1, STEPS + 1) for q in range(1 + s, 10 - s)]
LATE = [(s, q) for s in range(1, STEPS + 1) for q in [s, *range(10 - s, 14 - s)]]


def early_kernel(place_ref, coef_ref, own, out1, *refs):
    *pairs, kept, done = refs
    yl = place_ref[1]

    def load(s, q):
        if s:
            return kept[EARLY.index((s, q))]
        if q < 4:
            return out1[:, lanes_of(yl, q - 1)]
        if q < 7:
            return jnp.concatenate([pair[:, lanes_of(yl, q - 4)] for pair in pairs], axis=0)
        return own[:, lanes_of(yl, q - 7)]

    for n, (s, q) in enumerate(EARLY):
        x, before, after = load(s - 1, q), load(s - 1, q - 1), load(s - 1, q + 1)
        new = mirrored(coef_ref, place_ref, s - 1, q, x, before, after)
        if s == STEPS:
            done[...] = new.T
        else:
            kept[n] = new


def late_kernel(place_ref, coef_ref, own, out1, in1, out2, kept, done, *refs):
    *in2, out_ref, state = refs
    yl = place_ref[1]

    def rows_of(q):
        first = (place_of(yl, q) - HALO) * NLON
        return pl.ds(pl.multiple_of(first, NLON), NLON)

    def load(s, q):
        if (s, q) in LATE:
            return state[LATE.index((s, q))]
        if s:
            return kept[EARLY.index((s, q))]
        if q == 0:
            return out2[...]
        if q == WINDOW - 1:
            return in1[...]
        if q < 4:
            return out1[:, lanes_of(yl, q - 1)]
        if q < 10:
            return own[:, lanes_of(yl, q - 7)]
        return jnp.concatenate([part[:, lanes_of(yl, q - 10)] for part in in2], axis=0)

    out_ref[rows_of(EARLY[-1][1]), :] = done[...]
    for n, (s, q) in enumerate(LATE):
        x, before, after = load(s - 1, q), load(s - 1, q - 1), load(s - 1, q + 1)
        new = mirrored(coef_ref, place_ref, s - 1, q, x, before, after)
        if s == STEPS:
            out_ref[rows_of(q), :] = new.T
        else:
            state[n] = new


def cut_kernel(place_ref, cov_ref, own, near, *refs):
    *others, sems = refs
    yl = place_ref[1]
    cols = own.shape[0]
    mine = pl.ds(pl.multiple_of(yl * cols, cols), cols)
    inner = pl.ds(pl.multiple_of((1 - yl) * 2 * NLON, NLON), NLON)
    copies = []
    base = 0
    for n, other in enumerate(others):
        size = other.shape[0]
        theirs = pl.ds(pl.multiple_of((1 - yl) * cols + base, 8), size)
        copies.append(pltpu.make_async_copy(cov_ref.at[theirs, :], other, sems.at[2 + n]))
        base += size
    copies.append(pltpu.make_async_copy(cov_ref.at[mine, :], own, sems.at[0]))
    copies.append(pltpu.make_async_copy(cov_ref.at[mine, inner], near, sems.at[1]))
    for copy in copies:
        copy.start()
    for copy in copies:
        copy.wait()


def right_kernel(coef_ref, got_ref, out_ref, b0, b1, result, sems):
    half = got_ref.shape[0] // 2
    chunks = sems.shape[0]
    each = NLAT // chunks

    def first(lat):
        c, rest = divmod(lat, LATS_PLANE)
        yl, i = divmod(rest, LATS_DEV)
        return got_ref[yl * half + c, :, i * NLON : (i + 1) * NLON]

    zero = jnp.zeros((out_ref.shape[0], NLON), jnp.float32)
    bufs = (b0, b1)
    copies = []
    for s in range(STEPS):
        dst = bufs[(s + 1) % 2]
        load = first if s == 0 else lambda lat, src=bufs[s % 2]: src[lat]
        for lat in range(NLAT):
            south = load(lat - 1) if lat > 0 else zero
            north = load(lat + 1) if lat < NLAT - 1 else zero
            new = stencil(coef_ref[s, lat + HALO], load(lat), south, north)
            if s < STEPS - 1:
                dst[lat] = new
                continue
            result[:, lat * NLON : (lat + 1) * NLON] = new
            if (lat + 1) % each == 0:
                n = lat // each
                span = slice(n * each * NLON, (n + 1) * each * NLON)
                copy = pltpu.make_async_copy(result.at[:, span], out_ref.at[:, span], sems.at[n])
                copy.start()
                copies.append(copy)
    for copy in copies:
        copy.wait()


def shards(covariance, courant_x, courant_y, wind_index):
    planes = lax.axis_size("z")
    yl = lax.axis_index("yl")
    z = lax.axis_index("z")
    place = jnp.stack([z, yl]).astype(jnp.int32)
    cols = covariance.shape[0] // 2
    row = ("z", "yl")
    swap = [(r, r ^ 1) for r in range(2 * planes)]
    outward = [(r, r + (2 if r % 2 else -2)) for r in range(2 * planes)]
    outward = [(a, b) for a, b in outward if 0 <= b < 2 * planes]
    inward = [(b, a) for a, b in outward]
    smem = pl.BlockSpec(memory_space=pltpu.SMEM)
    vmem = pl.BlockSpec(memory_space=pltpu.VMEM)

    def shape(*dims):
        return jax.ShapeDtypeStruct(dims, jnp.float32)

    params = pltpu.CompilerParams(vmem_limit_bytes=VMEM_LIMIT)

    own, near, *others = pl.pallas_call(
        cut_kernel,
        in_specs=[smem, pl.BlockSpec(memory_space=pltpu.HBM)],
        out_specs=[vmem] * (2 + len(PARTS)),
        out_shape=[shape(cols, LATS_DEV * NLON), shape(cols, NLON)]
        + [shape(size, LATS_DEV * NLON) for size in PARTS],
        scratch_shapes=[pltpu.SemaphoreType.DMA((2 + len(PARTS),))],
        compiler_params=params,
        name="cut",
    )(place, covariance)
    pairs, in2 = [], []
    for other in others:
        pairs.append(lax.ppermute(other, row, swap))
    in1 = lax.ppermute(near, row, inward)
    out1 = lax.ppermute(own, row, outward)
    for pair in pairs:
        in2.append(lax.ppermute(pair, row, inward))
    far = [lax.dynamic_slice_in_dim(pair, yl * 2 * NLON, NLON, 1) for pair in pairs]
    out2 = lax.ppermute(jnp.concatenate(far, axis=0), row, outward)

    coefs = coefficients(courant_x, courant_y, wind_index)

    kept, done = pl.pallas_call(
        early_kernel,
        in_specs=[smem] + [vmem] * (3 + len(pairs)),
        out_specs=[vmem, vmem],
        out_shape=[shape(len(EARLY) - 1, cols, NLON), shape(NLON, cols)],
        compiler_params=params,
        name="early",
    )(place, coefs, own, out1, *pairs)
    propagated = pl.pallas_call(
        late_kernel,
        in_specs=[smem] + [vmem] * (7 + len(in2)),
        out_specs=vmem,
        out_shape=shape(LATS_PLANE * NLON, cols),
        scratch_shapes=[pltpu.VMEM((len(LATE) - 5, cols, NLON), jnp.float32)],
        compiler_params=params,
        name="late",
    )(place, coefs, own, out1, in1, out2, kept, done, *in2)

    group = ("yl", "x", "yh", "core")
    members = 2 * lax.axis_size("x") * lax.axis_size("yh") * lax.axis_size("core")
    rows_dev = LATS_PLANE * NLON // members
    sent = propagated.reshape(members, rows_dev, cols)
    got = lax.all_to_all(sent, group, split_axis=0, concat_axis=0, tiled=True)

    state = pltpu.VMEM((NLAT, rows_dev, NLON), jnp.float32)
    return pl.pallas_call(
        right_kernel,
        in_specs=[vmem, vmem],
        out_specs=pl.BlockSpec(memory_space=pl.ANY),
        out_shape=jax.ShapeDtypeStruct((rows_dev, NLAT * NLON), jnp.float32),
        scratch_shapes=[
            state,
            state,
            pltpu.VMEM((rows_dev, NLAT * NLON), jnp.float32),
            pltpu.SemaphoreType.DMA((4,)),
        ],
        compiler_params=pltpu.CompilerParams(vmem_limit_bytes=VMEM_LIMIT),
        name="right",
    )(coefs, got)


def solution(mesh):
    inner = Mesh(mesh.devices.reshape(16, 2, 4, 2, 2), ("z", "yl", "x", "yh", "core"))
    row, col = ("z", "yl"), ("x", "yh", "core")
    placed = (P(col, row), P(), P(), P())
    return jax.shard_map(
        shards, mesh=inner, in_specs=placed, out_specs=P(row + col, None), check_vma=False
    )
```

```python
import functools

import jax
import jax.numpy as jnp
from jax import lax
from jax.experimental import pallas as pl
from jax.experimental.pallas import tpu as pltpu
from jax.sharding import Mesh, PartitionSpec as P


NLAT = 96
NLON = 128
STEPS = 4
HALO = STEPS
DIFFUSIVITY = 0.05
LATS_DEV = 3
LATS_PLANE = 2 * LATS_DEV
WINDOW = LATS_PLANE + 2 * HALO
PARTS = (256, 128)
VMEM_LIMIT = 24 << 20


def coef_kernel(wind_ref, cx_ref, cy_ref, out_ref):
    flow_east = cx_ref[0]
    flow_north = cy_ref[0]
    east_pos = jnp.maximum(flow_east, 0.0)
    east_neg = jnp.minimum(flow_east, 0.0)
    north_pos = jnp.maximum(flow_north, 0.0)
    north_neg = jnp.minimum(flow_north, 0.0)
    centre = 1.0 - 4.0 * DIFFUSIVITY - (east_pos - east_neg) - (north_pos - north_neg)
    parts = (
        centre,
        east_pos + DIFFUSIVITY,
        DIFFUSIVITY - east_neg,
        north_pos + DIFFUSIVITY,
        DIFFUSIVITY - north_neg,
    )
    out_ref[...] = jnp.zeros_like(out_ref)
    for k, part in enumerate(parts):
        out_ref[0, pl.ds(8 * HALO + k, NLAT, stride=8), :] = part


def coefficients(courant_x, courant_y, wind_index):
    rows = 8 * (NLAT + 2 * HALO)
    out = pl.pallas_call(
        coef_kernel,
        grid_spec=pltpu.PrefetchScalarGridSpec(
            num_scalar_prefetch=1,
            grid=(STEPS,),
            in_specs=[
                pl.BlockSpec((1, NLAT, NLON), lambda s, wind: (wind[s], 0, 0)),
                pl.BlockSpec((1, NLAT, NLON), lambda s, wind: (wind[s], 0, 0)),
            ],
            out_specs=pl.BlockSpec((1, rows, NLON), lambda s, wind: (s, 0, 0)),
        ),
        out_shape=jax.ShapeDtypeStruct((STEPS, rows, NLON), jnp.float32),
        compiler_params=pltpu.CompilerParams(vmem_limit_bytes=VMEM_LIMIT),
        name="coefs",
    )(wind_index, courant_x, courant_y)
    return out.reshape(STEPS, NLAT + 2 * HALO, 8, NLON)


def stencil(coef, x, south, north):
    west = pltpu.roll(x, 1, 1)
    east = pltpu.roll(x, NLON - 1, 1)
    return (
        x * coef[0:1]
        + west * coef[1:2]
        + east * coef[2:3]
        + (south * coef[3:4] + north * coef[4:5])
    )


def lanes_of(yl, j):
    i = LATS_DEV - 1 - j + yl * (2 * j - LATS_DEV + 1)
    return pl.ds(pl.multiple_of(i * NLON, NLON), NLON)


def place_of(yl, q):
    return WINDOW - 1 - q + yl * (2 * q - WINDOW + 1)


def mirrored(coef_ref, place_ref, s, q, x, before, after):
    z = place_ref[0]
    yl = place_ref[1]
    lat = LATS_PLANE * z + place_of(yl, q)
    west = pltpu.roll(x, 1, 1)
    east = pltpu.roll(x, NLON - 1, 1)
    return (
        x * coef_ref[s, lat, 0:1, :]
        + west * coef_ref[s, lat, 1:2, :]
        + east * coef_ref[s, lat, 2:3, :]
        + (
            before * coef_ref[s, lat, pl.ds(4 - yl, 1), :]
            + after * coef_ref[s, lat, pl.ds(3 + yl, 1), :]
        )
    )


EARLY = [(s, q) for s in range(1, STEPS + 1) for q in range(1 + s, 10 - s)]
LATE = [(s, q) for s in range(1, STEPS + 1) for q in [s, *range(10 - s, 14 - s)]]


def early_kernel(place_ref, coef_ref, own, out1, *refs):
    *pairs, kept, done = refs
    yl = place_ref[1]

    def load(s, q):
        if s:
            return kept[EARLY.index((s, q))]
        if q < 4:
            return out1[:, lanes_of(yl, q - 1)]
        if q < 7:
            return jnp.concatenate([pair[:, lanes_of(yl, q - 4)] for pair in pairs], axis=0)
        return own[:, lanes_of(yl, q - 7)]

    for n, (s, q) in enumerate(EARLY):
        x, before, after = load(s - 1, q), load(s - 1, q - 1), load(s - 1, q + 1)
        new = mirrored(coef_ref, place_ref, s - 1, q, x, before, after)
        if s == STEPS:
            done[...] = new.T
        else:
            kept[n] = new


def late_kernel(base, place_ref, coef_ref, own, out1, in1, out2, in2, kept, done, *refs):
    *before_refs, out_ref, state = refs
    yl = place_ref[1]
    size = in2.shape[0]
    mine = slice(base, base + size)
    for ref in before_refs:
        out_ref[:, :base] = ref[...]

    def rows_of(q):
        first = (place_of(yl, q) - HALO) * NLON
        return pl.ds(pl.multiple_of(first, NLON), NLON)

    def load(s, q):
        if (s, q) in LATE:
            return state[LATE.index((s, q))]
        if s:
            return kept[EARLY.index((s, q)), mine, :]
        if q == 0:
            return out2[mine, :]
        if q == WINDOW - 1:
            return in1[mine, :]
        if q < 4:
            return out1[mine, lanes_of(yl, q - 1)]
        if q < 10:
            return own[mine, lanes_of(yl, q - 7)]
        return in2[:, lanes_of(yl, q - 10)]

    out_ref[rows_of(EARLY[-1][1]), mine] = done[:, mine]
    for n, (s, q) in enumerate(LATE):
        x, before, after = load(s - 1, q), load(s - 1, q - 1), load(s - 1, q + 1)
        new = mirrored(coef_ref, place_ref, s - 1, q, x, before, after)
        if s == STEPS:
            out_ref[rows_of(q), mine] = new.T
        else:
            state[n] = new


def pick_kernel(outer, place_ref, *refs):
    *pieces, out_ref = refs
    yl = place_ref[1]
    i = (LATS_DEV - 1) * (yl if outer else 1 - yl)
    lanes = pl.ds(pl.multiple_of(i * NLON, NLON), NLON)
    base = 0
    for piece in pieces:
        out_ref[base : base + piece.shape[0], :] = piece[:, lanes]
        base += piece.shape[0]


def right_kernel(coef_ref, got_ref, out_ref, b0, b1, result, sems):
    half = got_ref.shape[0] // 2
    chunks = sems.shape[0]
    each = NLAT // chunks

    def first(lat):
        c, rest = divmod(lat, LATS_PLANE)
        yl, i = divmod(rest, LATS_DEV)
        return got_ref[yl * half + c, :, i * NLON : (i + 1) * NLON]

    zero = jnp.zeros((out_ref.shape[0], NLON), jnp.float32)
    bufs = (b0, b1)
    copies = []
    for s in range(STEPS):
        dst = bufs[(s + 1) % 2]
        load = first if s == 0 else lambda lat, src=bufs[s % 2]: src[lat]
        for lat in range(NLAT):
            south = load(lat - 1) if lat > 0 else zero
            north = load(lat + 1) if lat < NLAT - 1 else zero
            new = stencil(coef_ref[s, lat + HALO], load(lat), south, north)
            if s < STEPS - 1:
                dst[lat] = new
                continue
            result[:, lat * NLON : (lat + 1) * NLON] = new
            if (lat + 1) % each == 0:
                n = lat // each
                span = slice(n * each * NLON, (n + 1) * each * NLON)
                copy = pltpu.make_async_copy(result.at[:, span], out_ref.at[:, span], sems.at[n])
                copy.start()
                copies.append(copy)
    for copy in copies:
        copy.wait()


def shards(covariance, courant_x, courant_y, wind_index):
    planes = lax.axis_size("z")
    yl = lax.axis_index("yl")
    z = lax.axis_index("z")
    place = jnp.stack([z, yl]).astype(jnp.int32)
    cols = covariance.shape[0] // 2
    row = ("z", "yl")
    swap = [(r, r ^ 1) for r in range(2 * planes)]
    devices = 2 * planes
    outward = [(r, r + (2 if r % 2 else -2)) for r in range(devices)]
    outward = [(a, b) for a, b in outward if 0 <= b < devices]
    inward = [(b, a) for a, b in outward]
    smem = pl.BlockSpec(memory_space=pltpu.SMEM)
    vmem = pl.BlockSpec(memory_space=pltpu.VMEM)

    def shape(*dims):
        return jax.ShapeDtypeStruct(dims, jnp.float32)

    params = pltpu.CompilerParams(vmem_limit_bytes=VMEM_LIMIT)

    def pick(outer, *pieces):
        return pl.pallas_call(
            functools.partial(pick_kernel, outer),
            in_specs=[smem] + [vmem] * len(pieces),
            out_specs=vmem,
            out_shape=shape(cols, NLON),
            compiler_params=params,
            name="pick",
        )(place, *pieces)

    own = lax.optimization_barrier(lax.dynamic_slice_in_dim(covariance, yl * cols, cols, 0))
    pairs, in2 = [], []
    base = (1 - yl) * cols
    for k, size in enumerate(PARTS):
        other = lax.dynamic_slice_in_dim(covariance, base, size, 0)
        base += size
        pairs.append(lax.ppermute(other, row, swap))
        in2.append(lax.ppermute(pairs[k], row, inward))
    in1 = lax.ppermute(pick(False, own), row, inward)
    out1 = lax.ppermute(own, row, outward)
    out2 = lax.ppermute(pick(True, *pairs), row, outward)

    coefs = coefficients(courant_x, courant_y, wind_index)

    kept, done = pl.pallas_call(
        early_kernel,
        in_specs=[smem] + [vmem] * (3 + len(pairs)),
        out_specs=[vmem, vmem],
        out_shape=[shape(len(EARLY) - 1, cols, NLON), shape(NLON, cols)],
        compiler_params=params,
        name="early",
    )(place, coefs, own, out1, *pairs)
    propagated = []
    base = 0
    for k, size in enumerate(PARTS):
        propagated = [
            pl.pallas_call(
                functools.partial(late_kernel, base),
                in_specs=[smem] + [vmem] * (8 + len(propagated)),
                out_specs=vmem,
                out_shape=shape(LATS_PLANE * NLON, base + size),
                scratch_shapes=[pltpu.VMEM((len(LATE) - 5, size, NLON), jnp.float32)],
                compiler_params=params,
            )(place, coefs, own, out1, in1, out2, in2[k], kept, done, *propagated)
        ]
        base += size

    group = ("yl", "x", "yh", "core")
    members = 2 * lax.axis_size("x") * lax.axis_size("yh") * lax.axis_size("core")
    rows_dev = LATS_PLANE * NLON // members
    sent = propagated[0].reshape(members, rows_dev, cols)
    got = lax.all_to_all(sent, group, split_axis=0, concat_axis=0, tiled=True)

    state = pltpu.VMEM((NLAT, rows_dev, NLON), jnp.float32)
    return pl.pallas_call(
        right_kernel,
        in_specs=[vmem, vmem],
        out_specs=pl.BlockSpec(memory_space=pl.ANY),
        out_shape=jax.ShapeDtypeStruct((rows_dev, NLAT * NLON), jnp.float32),
        scratch_shapes=[
            state,
            state,
            pltpu.VMEM((rows_dev, NLAT * NLON), jnp.float32),
            pltpu.SemaphoreType.DMA((8,)),
        ],
        compiler_params=pltpu.CompilerParams(vmem_limit_bytes=VMEM_LIMIT),
        name="right",
    )(coefs, got)


def solution(mesh):
    inner = Mesh(mesh.devices.reshape(16, 2, 4, 2, 2), ("z", "yl", "x", "yh", "core"))
    row, col = ("z", "yl"), ("x", "yh", "core")
    placed = (P(col, row), P(), P(), P())
    return jax.shard_map(
        shards, mesh=inner, in_specs=placed, out_specs=P(row + col, None), check_vma=False
    )
```
